128 devices in a mesh: row: 8 (over z, y_lo), col: 16 (over x, y_hi, core).
Axes of the slice: x: 4, y: 4 (y_hi: 2, y_lo: 2; y = y_hi * 2 + y_lo), z: 4, core: 2. Of those that a mesh axis runs over, the one named last changes fastest.
Arguments:
- seq_ids: int32 [4096], replicated, may hold values from 0 to 31, never falling along the last dimension, each value on 1 to 192 neighbouring positions
- attn_weights: float32 [4096, 64, 32], P(('row', 'col')), may hold values from 0.05 to 20
- values: bfloat16 [4096, 8192], P(('row', 'col')), may hold values from -6 to 6
- out_grads: bfloat16 [4096, 8192], P(('row', 'col')), may hold values from -2 to 2
- act_basis: bfloat16 [8192, 8192], P('row', 'col'), may hold values from -0.0625 to 0.0625
- grad_basis: bfloat16 [8192, 8192], P('col', 'row'), may hold values from -0.0625 to 0.0625
Outputs:
- eigenvalues: float32 [8192, 8192], P('row', 'col')
The draws below stay inside these ranges and needn't reach their ends.
Inputs may be any that keep to these rules, and one draw needn't show every extreme that they name: `seq_ids`: ids never fall along the tokens; each of the 32 sequences is one run of 1 to 192 tokens, and one has exactly 192.
All inputs are finite; a program needn't handle non-finite values.
Results may differ from the reference program's by a relative error of at most 0.014.
Values may be sent and summed in bfloat16 or wider, within the bound.
No kernel may reach another device: no remote copies, remote signals or barrier semaphores. Data moves between devices by JAX's collectives and lax.ppermute only.
A program may use at most 128 MiB of HBM per device.

```python
import math
import jax
import jax.numpy as jnp
import numpy as np
from jax import lax

HEADS = 64
HEAD = 128
D = 8192
WIN = 32
LONGEST = 192
TOKENS = 4096
SEQS = 32
N_ROW = 8
N_COL = 16


def levels(rng, shape, pieces, smallest, largest):
    factor_of, own = 1.0, jax.random.fold_in(rng, 6)
    for dim, parts in pieces:
        heights = jnp.exp(jax.random.uniform(jax.random.fold_in(own, dim), (parts,), jnp.float32, smallest / len(pieces), largest / len(pieces)))
        factor_of = factor_of * jnp.repeat(heights, shape[dim] // parts).reshape([-1 if axis == dim else 1 for axis in range(len(shape))])
    return factor_of


def split_up(amount, total, bound, slope):
    weights = [(1 << 20) // math.isqrt(grade ** slope) + 1 for grade in range(2, amount + 1)]
    rest, counts = total - bound - (amount - 1), [1] * (amount - 1)
    while rest > 0:
        movable = [i for i in range(amount - 1) if counts[i] < bound]
        mass, budget = sum([weights[i] for i in movable]), rest
        for i in movable:
            extra = min(bound - counts[i], max(1, budget * weights[i] // mass), rest)
            counts[i] = counts[i] + extra
            rest = rest - extra
    return np.array([bound] + counts)


def uneven_parts(rng, number_of, total, bound, lean):
    if number_of == 2:
        one = jax.random.randint(rng, (), max(1, total - bound), min(bound, total - 1) + 1)
        return jnp.stack([one, total - one])
    tallies = jnp.asarray(split_up(number_of, total, bound, lean), jnp.int32)
    pairs = (number_of - 1) // 2
    source_of, taker = tallies[1:1 + 2 * pairs:2], tallies[2:2 + 2 * pairs:2]
    margin = jnp.minimum(source_of - 1, bound - taker)
    passed = jax.random.randint(jax.random.fold_in(rng, 1), (pairs,), 0, 1 << 20) % (margin + 1)
    tallies = tallies.at[1:1 + 2 * pairs:2].set(source_of - passed).at[2:2 + 2 * pairs:2].set(taker + passed)
    return tallies[jax.random.permutation(jax.random.fold_in(rng, 2), number_of)]


def gaussian(key, shape, width, limit, pieces=(), held_as=jnp.bfloat16):
    gain = levels(key, shape, pieces, -0.22, 0.18) if pieces else 1.0
    result = jax.random.normal(key, shape, jnp.float32) * width * gain
    return jnp.minimum(jnp.maximum(result, -limit), limit).astype(held_as)


def setup_inputs(seed: int = 0) -> dict:
    key_list = jax.random.split(jax.random.key(seed), 7)
    seq_ids = jnp.searchsorted(jnp.cumsum(uneven_parts(key_list[0], SEQS, TOKENS, LONGEST, 1)), jnp.arange(TOKENS), side="right").astype(jnp.int32)
    attn_weights = jnp.clip(jnp.exp(math.log(20.0) - 5.9914645 * jax.random.uniform(key_list[1], (TOKENS, HEADS, WIN), jnp.float32) ** levels(key_list[1], (TOKENS, HEADS, WIN), ((0, 128),), -0.2, 0.2)), 0.05, 20.0)
    values = gaussian(key_list[2], (TOKENS, D), 1.0, 6.0, ((0, 128),))
    out_grads = gaussian(key_list[3], (TOKENS, D), 0.25, 2.0, ((0, 128),))
    act_basis = gaussian(key_list[4], (D, D), D ** -0.5, 0.0625, ((0, 8), (1, 16)))
    grad_basis = gaussian(key_list[5], (D, D), D ** -0.5, 0.0625, ((0, 16), (1, 8)))
    return {"seq_ids": seq_ids, "attn_weights": attn_weights, "values": values, "out_grads": out_grads, "act_basis": act_basis, "grad_basis": grad_basis}


def blocked_rotate(data, basis, blocks):
    size = D // blocks
    total = jnp.zeros((data.shape[0], basis.shape[1]), jnp.float32)
    for block in range(blocks):
        part = jnp.dot(data[:, block * size:(block + 1) * size].astype(jnp.float32), basis[block * size:(block + 1) * size, :].astype(jnp.float32))
        total = total + part.astype(jnp.bfloat16).astype(jnp.float32)
    return total.astype(jnp.bfloat16)


def reference(seq_ids, attn_weights, values, out_grads, act_basis, grad_basis):
    positions = jnp.arange(TOKENS, dtype=jnp.int32)
    offsets = jnp.arange(WIN, dtype=jnp.int32)
    key_pos = positions[:, None] - offsets[None, :]
    key_seg = seq_ids[jnp.clip(key_pos, 0, TOKENS - 1)]
    valid = jnp.logical_and(key_pos >= 0, key_seg == seq_ids[:, None]).astype(jnp.float32)
    masked = attn_weights * valid[:, None, :]
    probs = (masked / jnp.sum(masked, axis=2, keepdims=True)).astype(jnp.bfloat16)
    padded = jnp.concatenate([jnp.zeros((WIN, D), jnp.bfloat16), values], axis=0)
    mixed = jnp.zeros((TOKENS, HEADS, HEAD), jnp.float32)
    for step in range(WIN):
        shifted = padded[WIN - step:WIN - step + TOKENS].reshape(TOKENS, HEADS, HEAD).astype(jnp.float32)
        mixed = mixed + probs[:, :, step][:, :, None].astype(jnp.float32) * shifted
    inputs = mixed.reshape(TOKENS, D).astype(jnp.bfloat16)
    rot_inputs = blocked_rotate(inputs, act_basis, N_ROW)
    rot_grads = blocked_rotate(out_grads, grad_basis, N_COL)
    seq_range = jnp.arange(SEQS, dtype=jnp.int32)
    starts = jnp.sum((seq_ids[None, :] < seq_range[:, None]).astype(jnp.int32), axis=1).astype(jnp.int32)

    def accumulate(index, total):
        first = jnp.minimum(starts[index], TOKENS - LONGEST).astype(jnp.int32)
        grad_win = lax.dynamic_slice_in_dim(rot_grads, first, LONGEST, 0).astype(jnp.float32)
        act_win = lax.dynamic_slice_in_dim(rot_inputs, first, LONGEST, 0).astype(jnp.float32)
        seg_win = lax.dynamic_slice_in_dim(seq_ids, first, LONGEST, 0)
        grad_win = jnp.where((seg_win == index)[:, None], grad_win, jnp.float32(0.0))
        tile = jnp.dot(grad_win.T, act_win)
        return total + tile * tile

    total = lax.fori_loop(0, SEQS, accumulate, jnp.zeros((D, D), jnp.float32))
    return total / SEQS
```

```python
import jax
import jax.numpy as jnp
from jax import lax
from jax.experimental import pallas as pl
from jax.experimental.pallas import tpu as pltpu
from jax.sharding import Mesh, PartitionSpec as P

SEQS = 32
SPAN = 256
AXES = ("z", "w", "x", "v", "c")
SIZES = {"z": 4, "w": 2, "x": 4, "v": 2, "c": 2}


def shift(value, axis, steps=1):
    count = SIZES[axis]
    return lax.ppermute(value, axis, [(i, (i + steps) % count) for i in range(count)])


def exchange(pieces, axis):
    return [pieces[0]] + [shift(pieces[d], axis, d) for d in range(1, 4)]


def spread(own, ring, pair):
    half = own.shape[0] // 2
    out = []
    for block in (own, shift(own, pair)):
        below, above = shift(block, ring, 1), shift(block, ring, -1)
        first = shift(below[:half], ring, 1)
        second = shift(above[half:], ring, -1)
        out.append([block, below, above, first, second])
    return out


def collect(partial, ring):
    up = shift(partial[3], ring, 1)
    down = shift(partial[1], ring, -1)
    far = shift(partial[2], ring, 2)
    total = partial[0].astype(jnp.float32) + up.astype(jnp.float32)
    total = total + down.astype(jnp.float32) + far.astype(jnp.float32)
    return total.astype(jnp.bfloat16)


def attention(seq_ids, attn_weights, values, device):
    tok, width = values.shape
    heads, window = attn_weights.shape[1:]
    size = width // heads
    pairs = [(i, i + 1) for i in range(127)]
    previous = lax.ppermute(values, AXES, pairs)
    keys = jnp.concatenate([previous, values], axis=0).reshape(2 * tok, heads, size)
    offset = device * tok
    query_seg = lax.dynamic_slice_in_dim(seq_ids, offset, tok, 0)
    begin = jnp.sum((seq_ids[None, :] < query_seg[:, None]).astype(jnp.int32), axis=1)
    depth = offset + jnp.arange(tok, dtype=jnp.int32) - begin
    back = jnp.arange(window, dtype=jnp.int32)
    valid = (back[None, :] <= depth[:, None]).astype(jnp.float32)
    masked = attn_weights * valid[:, None, :]
    probs = (masked / jnp.sum(masked, axis=2, keepdims=True)).astype(jnp.bfloat16)
    local_key = tok + jnp.arange(tok, dtype=jnp.int32)[:, None] - back[None, :]
    selector = (
        local_key[:, :, None] == jnp.arange(2 * tok, dtype=jnp.int32)[None, None, :]
    ).astype(jnp.bfloat16)
    spread_probs = jnp.einsum(
        "phj,pjk->phk", probs, selector, preferred_element_type=jnp.float32
    ).astype(jnp.bfloat16)
    mixed = jnp.einsum("phk,khd->phd", spread_probs, keys, preferred_element_type=jnp.float32)
    return mixed.reshape(tok, width).astype(jnp.bfloat16)


def rotate(data, basis, ring_index, ring, pair):
    width = data.shape[1] // 4
    cuts = [
        lax.dynamic_slice_in_dim(data, ((ring_index + d) % 4) * width, width, 1) for d in range(4)
    ]
    own = jnp.stack(exchange(cuts, ring))
    other_ring, other_pair = pair
    blocks = spread(own, other_ring, other_pair)
    rows = []
    for below_own in blocks:
        block, below, above, first, second = below_own
        rows += [block, below, above, jnp.concatenate([first, second], axis=0)]
    stacked = jnp.stack(rows)
    flat = stacked.reshape(-1, width)
    partial = jnp.dot(flat, basis, preferred_element_type=jnp.float32).astype(jnp.bfloat16)
    partial = partial.reshape(8, 4, 32, -1).transpose(1, 0, 2, 3)
    return collect([partial[d] for d in range(4)], ring)


def tiles_kernel(starts, place, *refs):
    act_refs, grad_refs = refs[:10], refs[10:30]
    out, acts, grads, sems = refs[30:]
    z, w, x, v, c = (place[i] for i in range(5))
    ring = (0, 3, 1, 2)

    def row(zz, ww, xx, vv, cc):
        index = (((zz % 4) * 2 + ww) * 4 + xx % 4) * 4 + vv * 2 + cc
        return pl.ds(pl.multiple_of(index * 32, 32), 32)

    copies = []
    for jw in range(2):
        ww = w if jw == 0 else 1 - w
        for k in range(5):
            ref = act_refs[jw * 5 + k]
            zz = z + ring[min(k, 3)]
            dcs = (0, 1) if k < 3 else (k - 3,)
            for n, dc in enumerate(dcs):
                cc = c if dc == 0 else 1 - c
                for jv in range(2):
                    vv = v if jv == 0 else 1 - v
                    for r in range(4):
                        src = ref.at[n, jv * 4 + r]
                        dst = acts.at[row(zz, ww, x + ring[r], vv, cc)]
                        copies.append(pltpu.make_async_copy(src, dst, sems.at[0]))
    for dc in range(2):
        cc = c if dc == 0 else 1 - c
        for jv in range(2):
            vv = v if jv == 0 else 1 - v
            for k in range(5):
                ref = grad_refs[dc * 10 + jv * 5 + k]
                xx = x + ring[min(k, 3)]
                jws = (0, 1) if k < 3 else (k - 3,)
                for n, jw in enumerate(jws):
                    ww = w if jw == 0 else 1 - w
                    for r in range(4):
                        src = ref.at[n * 4 + r]
                        dst = grads.at[row(z + ring[r], ww, xx, vv, cc)]
                        copies.append(pltpu.make_async_copy(src, dst, sems.at[1]))
    for copy in copies:
        copy.start()
    out[...] = jnp.zeros_like(out)
    pltpu.make_async_copy(acts, acts, sems.at[0]).wait()
    pltpu.make_async_copy(grads, grads, sems.at[1]).wait()
    total, width = acts.shape
    part = 256

    def body(index, carry):
        first, last = starts[index], starts[index + 1]
        base = pl.multiple_of(jnp.minimum((first // 16) * 16, total - SPAN), 16)
        rows = base + lax.broadcasted_iota(jnp.int32, (SPAN, width), 0)
        act = acts[pl.ds(base, SPAN), :]
        act = jnp.where((rows >= first) & (rows < last), act, jnp.zeros_like(act))
        for m in range(out.shape[0] // part):
            span = slice(m * part, (m + 1) * part)
            tile = lax.dot_general(
                grads[pl.ds(base, SPAN), span],
                act,
                (((0,), (0,)), ((), ())),
                preferred_element_type=jnp.float32,
            )
            out[span, :] += tile * tile
        return carry

    lax.fori_loop(0, SEQS, body, 0)
    out[...] = out[...] * (1.0 / SEQS)


def tiles(starts, place, act_pieces, grad_pieces):
    total = starts.shape[0] and 4096
    return pl.pallas_call(
        tiles_kernel,
        out_shape=jax.ShapeDtypeStruct((1024, 512), jnp.float32),
        in_specs=[pl.BlockSpec(memory_space=pltpu.SMEM)] * 2
        + [pl.BlockSpec(memory_space=pl.ANY)] * 30,
        scratch_shapes=[
            pltpu.VMEM((total, 512), jnp.bfloat16),
            pltpu.VMEM((total, 1024), jnp.bfloat16),
            pltpu.SemaphoreType.DMA((2,)),
        ],
        compiler_params=pltpu.CompilerParams(vmem_limit_bytes=48 << 20),
        cost_estimate=pl.CostEstimate(
            flops=2 * SEQS * SPAN * 1024 * 512, bytes_accessed=14 << 20, transcendentals=0
        ),
        name="tiles",
    )(starts, place, *act_pieces, *grad_pieces)


def shards(seq_ids, attn_weights, values, out_grads, act_basis, grad_basis):
    z, w, x, v, c = (lax.axis_index(a) for a in AXES)
    device = (((z * 2 + w) * 4 + x) * 2 + v) * 2 + c

    grad_other = shift(grad_basis, "v")
    grad_mine = [grad_basis, shift(grad_basis, "c"), grad_other, shift(grad_other, "c")]
    grad_full = jnp.zeros((4,) + grad_basis.shape, grad_basis.dtype)
    for k, (dv, dc) in enumerate(((0, 0), (0, 1), (1, 0), (1, 1))):
        index = (v ^ dv) * 2 + (c ^ dc)
        grad_full = lax.dynamic_update_index_in_dim(grad_full, grad_mine[k], index, 0)
    grad_full = grad_full.reshape(-1, grad_basis.shape[1])
    act_other = shift(act_basis, "w")
    mine = jnp.concatenate([act_basis, shift(act_basis, "c")], axis=1)
    theirs = jnp.concatenate([act_other, shift(act_other, "c")], axis=1)
    act_full = jnp.where(
        w == 0, jnp.concatenate([mine, theirs], 0), jnp.concatenate([theirs, mine], 0)
    )

    inputs = attention(seq_ids, attn_weights, values, device)
    rot_grads = rotate(out_grads, grad_full, x, "x", ("z", "w"))
    rot_inputs = rotate(inputs, act_full, z, "z", ("x", "v"))

    half = rot_inputs.shape[2] // 2
    swapped = shift(rot_inputs[:, :, half:], "c")
    both = jnp.stack([rot_inputs[:, :, :half], swapped])
    act_pieces = [p for group in spread(both, "z", "w") for p in group]
    grad_pieces = [p for group in spread(rot_grads, "x", "v") for p in group]
    grad_pieces = grad_pieces + [shift(p, "c") for p in grad_pieces]

    marks = jnp.arange(SEQS + 1, dtype=jnp.int32)
    starts = jnp.sum((seq_ids[None, :] < marks[:, None]).astype(jnp.int32), axis=1)
    place = jnp.stack([z, w, x, v, c]).astype(jnp.int32)
    return tiles(starts, place, act_pieces, grad_pieces)


def solution(mesh):
    shape = tuple(SIZES[a] for a in AXES)
    fine = Mesh(mesh.devices.reshape(shape), AXES)
    every = P(AXES)
    row, col = ("z", "w"), ("x", "v", "c")
    return jax.shard_map(
        shards,
        mesh=fine,
        in_specs=(P(), every, every, every, P(row, col), P(col, row)),
        out_specs=P(row, col),
        check_vma=False,
    )
```
